32 devices in a mesh: seq: 8 (over y, x, core), tensor: 4 (over z).
Axes of the slice: x: 2, y: 2, z: 4, core: 2. Of those that a mesh axis runs over, the one named last changes fastest.
Arguments:
- queries: bfloat16 [1024, 4096], P('seq', 'tensor'), may hold values from -6 to 6
- keyvals: bfloat16 [16, 64, 1024], P('seq', 'tensor'), may hold values from -6 to 6
- reader_images: int32 [8, 3], replicated, may hold values from 0 to 15, as said below
- read_spans: int32 [2, 1024], P(None, 'seq'), may hold values from 0 to 3, as said below
- query_gain: float32 [128], replicated, may hold values from 1 to 2
- key_gain: float32 [128], replicated, may hold values from 1 to 2
- out_grad: bfloat16 [1024, 4096], P('seq', 'tensor'), may hold values from -6 to 6
Outputs:
- attention: bfloat16 [1024, 4096], P('seq', 'tensor')
- query_grad: bfloat16 [1024, 4096], P('seq', 'tensor')
- keyval_grad: bfloat16 [16, 64, 1024], P('seq', 'tensor')
The draws below stay inside these ranges and needn't reach their ends.
Inputs may be any that keep to these rules, and one draw needn't show every extreme that they name: `reader_images`: slot r of row j names an image held by text shard (j - r) modulo 8, that is one of images ((j - r) mod 8) * 2 to ((j - r) mod 8) * 2 + 1. A text token reads slots read_spans[0] to read_spans[1] - 1 of its shard's row of reader_images; one that reads none has 0 and 0; text shard j reads no slot r > j; some shard reads all 3 slots.
All inputs are finite; a program needn't handle non-finite values.
Results may differ from the reference program's by a relative error of at most 0.0095.
Values may be sent and summed in bfloat16 or wider, within the bound.
A program may use at most 64 MiB of HBM per device.

```python
import jax
import jax.numpy as jnp
from jax import lax

HD = 128
HEADS_DEV = 8
R_MAX = 3
IMG_DEV = 2
TOK_DEV = 128
SHARDS = 8
TOKENS = 1024
KV_HEADS = 4
HEADS = 32
NIMG = 16
IMG_TOK = 64


def layout_draw(key):
    folded = jax.random.fold_in(key, 4242)
    subkeys = jax.random.split(folded, 5)
    slot_index = jnp.arange(R_MAX, dtype=jnp.int32)
    reader_index = jnp.arange(SHARDS, dtype=jnp.int32)
    counts = jax.random.randint(subkeys[0], (SHARDS,), 1, R_MAX + 1, dtype=jnp.int32)
    forced = jax.random.randint(subkeys[1], (), R_MAX - 1, SHARDS, dtype=jnp.int32)
    counts = jnp.where(reader_index == forced, R_MAX, counts)
    counts = jnp.minimum(counts, reader_index + 1)
    holders = (reader_index[:, None] - slot_index[None, :]) % SHARDS
    picks = jax.random.randint(subkeys[2], (SHARDS, R_MAX), 0, IMG_DEV, dtype=jnp.int32)
    images = (holders * IMG_DEV + picks).astype(jnp.int32)
    spacing = TOK_DEV // R_MAX
    offsets = jax.random.randint(subkeys[3], (SHARDS, R_MAX), 0, spacing, dtype=jnp.int32)
    positions = slot_index[None, :] * spacing + offsets
    positions = jnp.where(slot_index[None, :] < counts[:, None], positions, TOK_DEV)
    doc_start = jax.random.randint(subkeys[4], (SHARDS, R_MAX), 0, 2, dtype=jnp.int32)
    doc_start = jnp.where(slot_index[None, :] == 0, 1, doc_start)
    token_index = jnp.arange(TOK_DEV, dtype=jnp.int32)
    slot_end = jnp.sum((positions[:, None, :] <= token_index[None, :, None]).astype(jnp.int32), axis=2)
    starts = slot_index[None, None, :] * doc_start[:, None, :] * (slot_index[None, None, :] < slot_end[:, :, None]).astype(jnp.int32)
    slot_begin = jnp.max(starts, axis=2)
    span_rows = jnp.stack([slot_begin.reshape(-1), slot_end.reshape(-1)], axis=0).astype(jnp.int32)
    return (images, span_rows)


def draw_reader_images(key, part):
    return layout_draw(key)[0]


def draw_read_spans(key, part):
    return layout_draw(key)[1]


def block_scale(own_key, shape, shards, least, largest):
    factor_of, own = 1.0, jax.random.fold_in(own_key, 6)
    for position, shards_of in shards:
        steps = jnp.exp(jax.random.uniform(jax.random.fold_in(own, position), (shards_of,), jnp.float32, least / len(shards), largest / len(shards)))
        factor_of = factor_of * jnp.repeat(steps, shape[position] // shards_of).reshape([-1 if axis == position else 1 for axis in range(len(shape))])
    return factor_of


def noise(stream_key, shape, scale, reach, cuts=(), kind=jnp.bfloat16):
    gain = block_scale(stream_key, shape, cuts, -0.22, 0.18) if cuts else 1.0
    drawn = jax.random.normal(stream_key, shape, jnp.float32) * scale * gain
    return jnp.minimum(jnp.maximum(drawn, -reach), reach).astype(kind)


def setup_inputs(seed: int = 0) -> dict:
    splits = jax.random.split(jax.random.key(seed), 8)
    return {
        "queries": noise(splits[0], (TOKENS, HEADS * HD), 1.0, 6.0, ((0, 8), (1, 4))),
        "keyvals": noise(splits[1], (NIMG, IMG_TOK, KV_HEADS * 2 * HD), 1.0, 6.0, ((0, 8), (1, 4))),
        "reader_images": draw_reader_images(jax.random.fold_in(splits[7], 71), 0),
        "read_spans": draw_read_spans(jax.random.fold_in(splits[7], 71), 0),
        "query_gain": jnp.clip(jax.random.uniform(splits[4], (HD,), jnp.float32, 1.0, 2.0), 1.0, 2.0),
        "key_gain": jnp.clip(jax.random.uniform(splits[5], (HD,), jnp.float32, 1.0, 2.0), 1.0, 2.0),
        "out_grad": noise(splits[6], (TOKENS, HEADS * HD), 1.0, 6.0, ((0, 8), (1, 4))),
    }


EPSILON = 1e-05

def norm_scale(values, weights):
    inverse = lax.rsqrt(lax.optimization_barrier(jnp.mean(values * values, axis=-1, keepdims=True)) + EPSILON)
    return values * inverse * weights

def norm_back(values, weights, upstream):
    inverse = lax.rsqrt(lax.optimization_barrier(jnp.mean(values * values, axis=-1, keepdims=True)) + EPSILON)
    scaled = weights * upstream
    return inverse * scaled - values * inverse * inverse * inverse * lax.optimization_barrier(jnp.mean(values * scaled, axis=-1, keepdims=True))

def rounded(values):
    return lax.optimization_barrier(values.astype(jnp.bfloat16)).astype(jnp.float32)

def reference(queries, keyvals, reader_images, read_spans, query_gain, key_gain, out_grad):
    score_scale = HD ** (-0.5)
    pair_rows = keyvals.reshape(NIMG, IMG_TOK, KV_HEADS, 2, HD)
    raw_keys = pair_rows[:, :, :, 0, :].astype(jnp.float32)
    key_hat = rounded(norm_scale(raw_keys, key_gain))
    values_all = pair_rows[:, :, :, 1, :].astype(jnp.float32)
    query_rows = queries.reshape(SHARDS, TOK_DEV, KV_HEADS, HEADS_DEV, HD)
    grad_rows = out_grad.reshape(SHARDS, TOK_DEV, KV_HEADS, HEADS_DEV, HD)
    begins = read_spans[0].reshape(SHARDS, TOK_DEV)
    finishes = read_spans[1].reshape(SHARDS, TOK_DEV)
    slot_ids = jnp.arange(R_MAX, dtype=jnp.int32)

    def shard_step(totals, inputs):
        query_block, grad_block, begin_slot, finish, images = inputs
        query_float = query_block.astype(jnp.float32)
        query_hat = rounded(norm_scale(query_float, query_gain))
        keys_used = key_hat[images]
        vals_used = values_all[images]
        slot_masks = ((begin_slot[None, :] <= slot_ids[:, None]) & (slot_ids[:, None] < finish[None, :])).astype(jnp.float32)
        no_image = 1.0 - lax.optimization_barrier(jnp.max(slot_masks, axis=0))
        scores = jnp.einsum('tcad,rucd->rtcau', query_hat, keys_used) * score_scale
        weights = jnp.exp(scores) * slot_masks[:, :, None, None, None]
        denominator = lax.optimization_barrier(jnp.sum(weights, axis=(0, 4))) + no_image[:, None, None]
        numerator = jnp.einsum('rtcau,rucd->tcad', rounded(weights), vals_used)
        attended = rounded(numerator / denominator[..., None])
        probabilities = weights / denominator[None, :, :, :, None]
        grad_float = grad_block.astype(jnp.float32)
        dot_rows = lax.optimization_barrier(jnp.sum(grad_float * attended, axis=-1))
        grad_probs = jnp.einsum('tcad,rucd->rtcau', grad_float, vals_used)
        grad_scores = rounded(probabilities * (grad_probs - dot_rows[None, :, :, :, None]))
        grad_query_hat = jnp.einsum('rtcau,rucd->tcad', grad_scores, keys_used) * score_scale
        grad_query = norm_back(query_float, query_gain, grad_query_hat).astype(jnp.bfloat16)
        grad_key_hat = jnp.einsum('rtcau,tcad->rucd', grad_scores, query_hat) * score_scale
        grad_value = jnp.einsum('rtcau,tcad->rucd', rounded(probabilities), grad_float)
        totals = totals.at[images].add(jnp.stack([grad_key_hat, grad_value], axis=3))
        return (totals, (attended.astype(jnp.bfloat16), grad_query))
    zero_totals = jnp.zeros((NIMG, IMG_TOK, KV_HEADS, 2, HD), jnp.float32)
    totals, outputs = lax.scan(shard_step, zero_totals, (query_rows, grad_rows, begins, finishes, reader_images))
    attended, grad_query = outputs
    grad_keys = norm_back(raw_keys, key_gain, totals[:, :, :, 0, :])
    keyval_grad = jnp.stack([grad_keys, totals[:, :, :, 1, :]], axis=3).astype(jnp.bfloat16)
    keyval_grad = keyval_grad.reshape(NIMG, IMG_TOK, KV_HEADS * 2 * HD)
    return (attended.reshape(TOKENS, HEADS * HD), grad_query.reshape(TOKENS, HEADS * HD), keyval_grad)
```

```python
import functools

import jax
import jax.numpy as jnp
from jax import lax
from jax.experimental import pallas as pl
from jax.experimental.pallas import tpu as pltpu
from jax.sharding import PartitionSpec as P

EPSILON = 1e-05
MESH = pl.DeviceIdType.MESH
F32 = jnp.float32
BF16 = jnp.bfloat16
ROWS = (((1,), (1,)), ((), ()))
COLUMNS = (((0,), (0,)), ((), ()))


def inverse_of(values):
    return lax.rsqrt(jnp.mean(values * values, axis=-1, keepdims=True) + EPSILON)


def dot(a, b, dims=None):
    if dims is None:
        return jnp.dot(a, b, preferred_element_type=F32)
    return lax.dot_general(a, b, dims, preferred_element_type=F32)


def kernel(
    seq_count, tensor_count,
    images_ref, spans_ref, query_gain_ref, key_gain_ref, kv_hbm, q_hbm, do_hbm,
    att_hbm, qg_hbm, kvg_hbm,
    kv, q, do, qhat, send, arrive, gsend, garrive, wb, dsb, att, qg, kvg, denoms,
    in_sem, out_sem, send_sem, recv_sem, gsend_sem, grecv_sem,
):
    s = lax.axis_index("seq")
    t = lax.axis_index("tensor")
    slots, _, sub, width2 = arrive.shape
    width = width2 // 2
    image_count = kv.shape[0]
    tokens = q.shape[0]
    group = q.shape[1] // width
    image_rows = tensor_count * sub
    all_rows = slots * image_rows
    scale = width ** (-0.5)

    def ring(k):
        return lax.rem(t + k, tensor_count)

    kv_in = pltpu.make_async_copy(kv_hbm, kv, in_sem.at[0])
    q_in = pltpu.make_async_copy(q_hbm, q, in_sem.at[1])
    do_in = pltpu.make_async_copy(do_hbm, do, in_sem.at[2])
    kv_in.start()
    q_in.start()
    do_in.start()

    barrier = pltpu.get_barrier_semaphore()
    for shift in range(1 - slots, slots):

        def greet(shift=shift):
            for k in range(tensor_count):
                if shift or k:
                    pl.semaphore_signal(
                        barrier, inc=1, device_id=(s + shift, ring(k)), device_id_type=MESH
                    )

        if shift == 0:
            greet()
        else:
            pl.when((s + shift >= 0) & (s + shift < seq_count))(greet)

    picks = []
    for r in range(slots):
        reader = jnp.minimum(s + r, seq_count - 1)
        pick = images_ref[reader, r] - s * image_count
        picks.append(jnp.clip(pick, 0, image_count - 1))

    kv_in.wait()
    for r in range(slots):
        chosen = kv[picks[r]]
        for k in range(tensor_count):
            send[r, k] = chosen[:, k * width2 : (k + 1) * width2]
    arrive[0, t] = send[0, t]
    for r in range(1, slots):

        @pl.when(s < r)
        def _(r=r):
            arrive[r] = jnp.zeros(arrive.shape[1:], BF16)

        @pl.when(s + r >= seq_count)
        def _(r=r):
            garrive[r] = jnp.zeros(garrive.shape[1:], BF16)

    near = jnp.minimum(s, slots - 1) + jnp.minimum(seq_count - 1 - s, slots - 1) + 1
    pl.semaphore_wait(barrier, near * tensor_count - 1)

    def forward(r, k, slot):
        return pltpu.make_async_remote_copy(
            src_ref=send.at[r, ring(k)], dst_ref=arrive.at[r, slot],
            send_sem=send_sem.at[r, k], recv_sem=recv_sem.at[r, k],
            device_id=(s + r, ring(k)), device_id_type=MESH,
        )

    def backward(r, k, slot):
        return pltpu.make_async_remote_copy(
            src_ref=gsend.at[r, ring(k)], dst_ref=garrive.at[r, slot],
            send_sem=gsend_sem.at[r, k], recv_sem=grecv_sem.at[r, k],
            device_id=(s - r, ring(k)), device_id_type=MESH,
        )

    def each(r, condition, body):
        def run():
            for k in reversed(range(tensor_count)):
                if r or k:
                    body(k)

        if r == 0:
            run()
        else:
            pl.when(condition)(run)

    def from_ring(k):
        return lax.rem(t + tensor_count - k, tensor_count)

    for r in reversed(range(slots)):
        each(r, s + r < seq_count, lambda k, r=r: forward(r, k, t).start())

    query_gain = query_gain_ref[...]
    key_gain = key_gain_ref[...]
    q_in.wait()
    for a in range(group):
        qf = q[:, a * width : (a + 1) * width].astype(F32)
        qhat[a] = (qf * inverse_of(qf) * query_gain).astype(BF16)
    do_in.wait()

    begins = spans_ref[0:1, :]
    ends = spans_ref[1:2, :]
    masks = [((begins <= r) & (r < ends)).astype(F32) for r in range(slots)]
    no_image = 1.0 - functools.reduce(jnp.maximum, masks)
    mask = jnp.concatenate(
        [jnp.broadcast_to(m, (image_rows, tokens)) for m in masks], axis=0
    )

    for r in range(slots):
        each(r, s >= r, lambda k, r=r: forward(r, k, from_ring(k)).wait_recv())

    arrived = arrive[...].reshape(all_rows, width2)
    keys = arrived[:, :width].astype(F32)
    values = arrived[:, width:]
    key_hat = (keys * inverse_of(keys) * key_gain).astype(BF16)

    grad_key = jnp.zeros((all_rows, width), F32)
    grad_value = jnp.zeros((all_rows, width), F32)
    for a in range(group):
        grad_out = do[:, a * width : (a + 1) * width]
        query = qhat[a]
        weights = jnp.exp(dot(key_hat, query, ROWS) * scale) * mask
        denominator = jnp.sum(weights, axis=0, keepdims=True) + no_image
        probs = weights * (1.0 / denominator)
        grad_probs = dot(values, grad_out, ROWS)
        row_dot = jnp.sum(probs * grad_probs, axis=0, keepdims=True)
        score_grad = (probs * (grad_probs - row_dot)).astype(BF16)
        wb[a] = weights.astype(BF16)
        dsb[a] = score_grad
        denoms[a : a + 1, :] = denominator
        grad_key = grad_key + dot(score_grad, query)
        grad_value = grad_value + dot(probs.astype(BF16), grad_out)
    piece = (slots, tensor_count, sub, width)
    gsend[:, :, :, :width] = (grad_key * scale).astype(BF16).reshape(piece)
    gsend[:, :, :, width:] = grad_value.astype(BF16).reshape(piece)

    for r in reversed(range(slots)):
        each(r, s >= r, lambda k, r=r: backward(r, k, t).start())
    garrive[0, t] = gsend[0, t]

    padded = jnp.concatenate(
        [denoms[...], jnp.ones((tokens - group, tokens), F32)], axis=0
    ) if tokens > group else denoms[...]
    columns = 1.0 / jnp.transpose(padded)
    for a in range(group):
        part = slice(a * width, (a + 1) * width)
        numerator = dot(wb[a], values, COLUMNS)
        att[:, part] = (numerator * columns[:, a : a + 1]).astype(BF16)
    att_out = pltpu.make_async_copy(att, att_hbm, out_sem.at[0])
    att_out.start()
    for a in range(group):
        part = slice(a * width, (a + 1) * width)
        scaled = query_gain * (dot(dsb[a], key_hat, COLUMNS) * scale)
        qf = q[:, part].astype(F32)
        inverse = inverse_of(qf)
        mean = jnp.mean(qf * scaled, axis=-1, keepdims=True)
        qg[:, part] = (inverse * scaled - qf * (inverse * inverse * inverse * mean)).astype(BF16)
    qg_out = pltpu.make_async_copy(qg, qg_hbm, out_sem.at[1])
    qg_out.start()

    for r in range(slots):
        each(r, s + r < seq_count, lambda k, r=r: backward(r, k, from_ring(k)).wait_recv())

    for i in range(image_count):
        chosen = [(picks[r] == i) & (s + r < seq_count) for r in range(slots)]
        for h in range(tensor_count):
            total = jnp.zeros((sub, width2), F32)
            for r in range(slots):
                total = total + jnp.where(chosen[r], garrive[r, h].astype(F32), 0.0)
            start = h * width2
            raw = kv[i, :, start : start + width].astype(F32)
            inverse = inverse_of(raw)
            scaled = key_gain * total[:, :width]
            mean = jnp.mean(raw * scaled, axis=-1, keepdims=True)
            kvg[i, :, start : start + width] = (
                inverse * scaled - raw * (inverse * inverse * inverse * mean)
            ).astype(BF16)
            kvg[i, :, start + width : start + width2] = total[:, width:].astype(BF16)
    kvg_out = pltpu.make_async_copy(kvg, kvg_hbm, out_sem.at[2])
    kvg_out.start()

    for r in range(slots):
        each(r, s + r < seq_count, lambda k, r=r: forward(r, k, t).wait_send())
        each(r, s >= r, lambda k, r=r: backward(r, k, t).wait_send())
    att_out.wait()
    qg_out.wait()
    kvg_out.wait()


def local(seq_count, tensor_count, queries, keyvals, reader_images, read_spans, query_gain, key_gain, out_grad):
    width = query_gain.shape[0]
    tokens, columns = queries.shape
    group = columns // width
    image_count, sub, _ = keyvals.shape
    slots = reader_images.shape[1]
    rows = slots * tensor_count * sub
    pieces = (slots, tensor_count, sub, 2 * width)
    whole = pl.BlockSpec(memory_space=pltpu.VMEM)
    placed = pl.BlockSpec(memory_space=pl.ANY)
    pairs = (slots, tensor_count)
    return pl.pallas_call(
        functools.partial(kernel, seq_count, tensor_count),
        out_shape=(
            jax.ShapeDtypeStruct(queries.shape, BF16),
            jax.ShapeDtypeStruct(queries.shape, BF16),
            jax.ShapeDtypeStruct(keyvals.shape, BF16),
        ),
        in_specs=[pl.BlockSpec(memory_space=pltpu.SMEM), whole, whole, whole, placed, placed, placed],
        out_specs=(placed, placed, placed),
        scratch_shapes=[
            pltpu.VMEM(keyvals.shape, BF16),
            pltpu.VMEM(queries.shape, BF16),
            pltpu.VMEM(queries.shape, BF16),
            pltpu.VMEM((group, tokens, width), BF16),
            pltpu.VMEM(pieces, BF16),
            pltpu.VMEM(pieces, BF16),
            pltpu.VMEM(pieces, BF16),
            pltpu.VMEM(pieces, BF16),
            pltpu.VMEM((group, rows, tokens), BF16),
            pltpu.VMEM((group, rows, tokens), BF16),
            pltpu.VMEM(queries.shape, BF16),
            pltpu.VMEM(queries.shape, BF16),
            pltpu.VMEM(keyvals.shape, BF16),
            pltpu.VMEM((group, tokens), F32),
            pltpu.SemaphoreType.DMA((3,)),
            pltpu.SemaphoreType.DMA((3,)),
            pltpu.SemaphoreType.DMA(pairs),
            pltpu.SemaphoreType.DMA(pairs),
            pltpu.SemaphoreType.DMA(pairs),
            pltpu.SemaphoreType.DMA(pairs),
        ],
        compiler_params=pltpu.CompilerParams(collective_id=0, has_side_effects=True),
        name="cross_attention",
    )(
        reader_images, read_spans, query_gain.reshape(1, width), key_gain.reshape(1, width),
        keyvals, queries, out_grad,
    )


def solution(mesh):
    placed = (
        P("seq", "tensor"),
        P("seq", "tensor", None),
        P(),
        P(None, "seq"),
        P(),
        P(),
        P("seq", "tensor"),
    )
    return jax.shard_map(
        functools.partial(local, mesh.shape["seq"], mesh.shape["tensor"]),
        mesh=mesh,
        in_specs=placed,
        out_specs=(P("seq", "tensor"), P("seq", "tensor"), P("seq", "tensor", None)),
        check_vma=False,
    )
```

```python
import functools

import jax
import jax.numpy as jnp
from jax import lax
from jax.experimental import pallas as pl
from jax.experimental.pallas import tpu as pltpu
from jax.sharding import PartitionSpec as P

EPSILON = 1e-05
MESH = pl.DeviceIdType.MESH
F32 = jnp.float32
BF16 = jnp.bfloat16
ROWS = (((1,), (1,)), ((), ()))
COLUMNS = (((0,), (0,)), ((), ()))


def inverse_of(values):
    return lax.rsqrt(jnp.mean(values * values, axis=-1, keepdims=True) + EPSILON)


def dot(a, b, dims=None):
    if dims is None:
        return jnp.dot(a, b, preferred_element_type=F32)
    return lax.dot_general(a, b, dims, preferred_element_type=F32)


def kernel(
    seq_count, tensor_count,
    images_hbm, spans_hbm, query_gain_hbm, key_gain_hbm, kv_hbm, q_hbm, do_hbm,
    att_hbm, qg_hbm, kvg_hbm,
    images_ref, spans_ref, query_gain_ref, key_gain_ref, kv, q, do, qhat, send, arrive, gsend, garrive, wb, dsb, att, qg, kvg, denoms,
    in_sem, out_sem, send_sem, recv_sem, gsend_sem, grecv_sem,
):
    s = lax.axis_index("seq")
    t = lax.axis_index("tensor")
    slots, _, sub, width2 = arrive.shape
    width = width2 // 2
    image_count = kv.shape[0]
    tokens = q.shape[0]
    group = q.shape[1] // width
    image_rows = tensor_count * sub
    all_rows = slots * image_rows
    scale = width ** (-0.5)

    def ring(k):
        return lax.rem(t + k, tensor_count)

    kv_in = pltpu.make_async_copy(kv_hbm, kv, in_sem.at[0])
    q_in = pltpu.make_async_copy(q_hbm, q, in_sem.at[1])
    do_in = pltpu.make_async_copy(do_hbm, do, in_sem.at[2])
    small = (
        (images_hbm, images_ref), (spans_hbm, spans_ref),
        (query_gain_hbm, query_gain_ref), (key_gain_hbm, key_gain_ref),
    )
    small_in = [
        pltpu.make_async_copy(a, b, in_sem.at[3 + i]) for i, (a, b) in enumerate(small)
    ]
    small_in[0].start()
    kv_in.start()
    for copy in small_in[1:]:
        copy.start()
    q_in.start()
    do_in.start()

    barrier = pltpu.get_barrier_semaphore()
    for shift in range(1 - slots, slots):

        def greet(shift=shift):
            for k in range(tensor_count):
                if shift or k:
                    pl.semaphore_signal(
                        barrier, inc=1, device_id=(s + shift, ring(k)), device_id_type=MESH
                    )

        if shift == 0:
            greet()
        else:
            pl.when((s + shift >= 0) & (s + shift < seq_count))(greet)

    small_in[0].wait()
    picks = []
    for r in range(slots):
        reader = jnp.minimum(s + r, seq_count - 1)
        pick = images_ref[r, reader] - s * image_count
        picks.append(jnp.clip(pick, 0, image_count - 1))

    kv_in.wait()
    for r in range(slots):
        chosen = kv[picks[r]]
        for k in range(tensor_count):
            send[r, k] = chosen[:, k * width2 : (k + 1) * width2]
    arrive[0, t] = send[0, t]
    for r in range(1, slots):

        @pl.when(s < r)
        def _(r=r):
            arrive[r] = jnp.zeros(arrive.shape[1:], BF16)

        @pl.when(s + r >= seq_count)
        def _(r=r):
            garrive[r] = jnp.zeros(garrive.shape[1:], BF16)

    near = jnp.minimum(s, slots - 1) + jnp.minimum(seq_count - 1 - s, slots - 1) + 1
    pl.semaphore_wait(barrier, near * tensor_count - 1)

    def forward(r, k, slot):
        return pltpu.make_async_remote_copy(
            src_ref=send.at[r, ring(k)], dst_ref=arrive.at[r, slot],
            send_sem=send_sem.at[r, k], recv_sem=recv_sem.at[r, k],
            device_id=(s + r, ring(k)), device_id_type=MESH,
        )

    def backward(r, k, slot):
        return pltpu.make_async_remote_copy(
            src_ref=gsend.at[r, ring(k)], dst_ref=garrive.at[r, slot],
            send_sem=gsend_sem.at[r, k], recv_sem=grecv_sem.at[r, k],
            device_id=(s - r, ring(k)), device_id_type=MESH,
        )

    def each(r, condition, body):
        def run():
            for k in reversed(range(tensor_count)):
                if r or k:
                    body(k)

        if r == 0:
            run()
        else:
            pl.when(condition)(run)

    def from_ring(k):
        return lax.rem(t + tensor_count - k, tensor_count)

    for r in reversed(range(slots)):
        each(r, s + r < seq_count, lambda k, r=r: forward(r, k, t).start())

    for copy in small_in[1:]:
        copy.wait()
    query_gain = query_gain_ref[...]
    key_gain = key_gain_ref[...]
    q_in.wait()
    for a in range(group):
        qf = q[:, a * width : (a + 1) * width].astype(F32)
        qhat[a] = (qf * inverse_of(qf) * query_gain).astype(BF16)
    do_in.wait()

    begins = spans_ref[0:1, :]
    ends = spans_ref[1:2, :]
    masks = [((begins <= r) & (r < ends)).astype(F32) for r in range(slots)]
    no_image = 1.0 - functools.reduce(jnp.maximum, masks)
    mask = jnp.concatenate(
        [jnp.broadcast_to(m, (image_rows, tokens)) for m in masks], axis=0
    )

    for r in range(slots):
        each(r, s >= r, lambda k, r=r: forward(r, k, from_ring(k)).wait_recv())

    arrived = arrive[...].reshape(all_rows, width2)
    keys = arrived[:, :width].astype(F32)
    values = arrived[:, width:]
    key_hat = (keys * inverse_of(keys) * key_gain).astype(BF16)

    grad_key = jnp.zeros((all_rows, width), F32)
    grad_value = jnp.zeros((all_rows, width), F32)
    for a in range(group):
        grad_out = do[:, a * width : (a + 1) * width]
        query = qhat[a]
        weights = jnp.exp(dot(key_hat, query, ROWS) * scale) * mask
        denominator = jnp.sum(weights, axis=0, keepdims=True) + no_image
        probs = weights * (1.0 / denominator)
        grad_probs = dot(values, grad_out, ROWS)
        row_dot = jnp.sum(probs * grad_probs, axis=0, keepdims=True)
        score_grad = (probs * (grad_probs - row_dot)).astype(BF16)
        wb[a] = weights.astype(BF16)
        dsb[a] = score_grad
        denoms[a : a + 1, :] = denominator
        grad_key = grad_key + dot(score_grad, query)
        grad_value = grad_value + dot(probs.astype(BF16), grad_out)
    piece = (slots, tensor_count, sub, width)
    gsend[:, :, :, :width] = (grad_key * scale).astype(BF16).reshape(piece)
    gsend[:, :, :, width:] = grad_value.astype(BF16).reshape(piece)

    for r in reversed(range(slots)):
        each(r, s >= r, lambda k, r=r: backward(r, k, t).start())
    garrive[0, t] = gsend[0, t]

    padded = jnp.concatenate(
        [denoms[...], jnp.ones((tokens - group, tokens), F32)], axis=0
    ) if tokens > group else denoms[...]
    columns = 1.0 / jnp.transpose(padded)
    for a in range(group):
        part = slice(a * width, (a + 1) * width)
        numerator = dot(wb[a], values, COLUMNS)
        att[:, part] = (numerator * columns[:, a : a + 1]).astype(BF16)
    att_out = pltpu.make_async_copy(att, att_hbm, out_sem.at[0])
    att_out.start()
    for a in range(group):
        part = slice(a * width, (a + 1) * width)
        scaled = query_gain * (dot(dsb[a], key_hat, COLUMNS) * scale)
        qf = q[:, part].astype(F32)
        inverse = inverse_of(qf)
        mean = jnp.mean(qf * scaled, axis=-1, keepdims=True)
        qg[:, part] = (inverse * scaled - qf * (inverse * inverse * inverse * mean)).astype(BF16)
    qg_out = pltpu.make_async_copy(qg, qg_hbm, out_sem.at[1])
    qg_out.start()

    for r in range(slots):
        each(r, s + r < seq_count, lambda k, r=r: backward(r, k, from_ring(k)).wait_recv())

    for i in range(image_count):
        chosen = [(picks[r] == i) & (s + r < seq_count) for r in range(slots)]
        for h in range(tensor_count):
            total = jnp.zeros((sub, width2), F32)
            for r in range(slots):
                total = total + jnp.where(chosen[r], garrive[r, h].astype(F32), 0.0)
            start = h * width2
            raw = kv[i, :, start : start + width].astype(F32)
            inverse = inverse_of(raw)
            scaled = key_gain * total[:, :width]
            mean = jnp.mean(raw * scaled, axis=-1, keepdims=True)
            kvg[i, :, start : start + width] = (
                inverse * scaled - raw * (inverse * inverse * inverse * mean)
            ).astype(BF16)
            kvg[i, :, start + width : start + width2] = total[:, width:].astype(BF16)
    kvg_out = pltpu.make_async_copy(kvg, kvg_hbm, out_sem.at[2])
    kvg_out.start()

    for r in range(slots):
        each(r, s + r < seq_count, lambda k, r=r: forward(r, k, t).wait_send())
        each(r, s >= r, lambda k, r=r: backward(r, k, t).wait_send())
    att_out.wait()
    qg_out.wait()
    kvg_out.wait()


def hand_out(att_in, qg_in, kvg_in, att, qg, kvg, sems):
    pairs = ((att_in, att), (qg_in, qg), (kvg_in, kvg))
    copies = [pltpu.make_async_copy(a, b, sems.at[i]) for i, (a, b) in enumerate(pairs)]
    for copy in copies:
        copy.start()
    for copy in copies:
        copy.wait()


def local(seq_count, tensor_count, queries, keyvals, reader_images, read_spans, query_gain, key_gain, out_grad):
    width = query_gain.shape[0]
    tokens, columns = queries.shape
    group = columns // width
    image_count, sub, _ = keyvals.shape
    slots = reader_images.shape[1]
    rows = slots * tensor_count * sub
    pieces = (slots, tensor_count, sub, 2 * width)
    held = pl.BlockSpec(memory_space=pltpu.HBM)
    placed = pl.BlockSpec(memory_space=pl.ANY)
    pairs = (slots, tensor_count)
    operands = (
        reader_images.T, read_spans, query_gain.reshape(1, width), key_gain.reshape(1, width),
        keyvals, queries, out_grad,
    )
    results = pl.pallas_call(
        functools.partial(kernel, seq_count, tensor_count),
        out_shape=(
            jax.ShapeDtypeStruct(queries.shape, BF16),
            jax.ShapeDtypeStruct(queries.shape, BF16),
            jax.ShapeDtypeStruct(keyvals.shape, BF16),
        ),
        in_specs=[held] * 7,
        out_specs=(placed, placed, placed),
        scratch_shapes=[
            pltpu.SMEM(reader_images.shape[::-1], jnp.int32),
            pltpu.VMEM(read_spans.shape, jnp.int32),
            pltpu.VMEM((1, width), F32),
            pltpu.VMEM((1, width), F32),
            pltpu.VMEM(keyvals.shape, BF16),
            pltpu.VMEM(queries.shape, BF16),
            pltpu.VMEM(queries.shape, BF16),
            pltpu.VMEM((group, tokens, width), BF16),
            pltpu.VMEM(pieces, BF16),
            pltpu.VMEM(pieces, BF16),
            pltpu.VMEM(pieces, BF16),
            pltpu.VMEM(pieces, BF16),
            pltpu.VMEM((group, rows, tokens), BF16),
            pltpu.VMEM((group, rows, tokens), BF16),
            pltpu.VMEM(queries.shape, BF16),
            pltpu.VMEM(queries.shape, BF16),
            pltpu.VMEM(keyvals.shape, BF16),
            pltpu.VMEM((group, tokens), F32),
            pltpu.SemaphoreType.DMA((7,)),
            pltpu.SemaphoreType.DMA((3,)),
            pltpu.SemaphoreType.DMA(pairs),
            pltpu.SemaphoreType.DMA(pairs),
            pltpu.SemaphoreType.DMA(pairs),
            pltpu.SemaphoreType.DMA(pairs),
        ],
        compiler_params=pltpu.CompilerParams(collective_id=0, has_side_effects=True, vmem_limit_bytes=24 * 2**20),
        name="cross_attention",
    )(*[pltpu.with_memory_space_constraint(operand, pltpu.HBM) for operand in operands])
    return pl.pallas_call(
        hand_out,
        out_shape=tuple(jax.ShapeDtypeStruct(r.shape, r.dtype) for r in results),
        in_specs=[placed] * len(results),
        out_specs=(placed,) * len(results),
        scratch_shapes=[pltpu.SemaphoreType.DMA((len(results),))],
        compiler_params=pltpu.CompilerParams(vmem_limit_bytes=2**20),
        name="hand_out",
    )(*results)


def solution(mesh):
    placed = (
        P("seq", "tensor"),
        P("seq", "tensor", None),
        P(),
        P(None, "seq"),
        P(),
        P(),
        P("seq", "tensor"),
    )
    return jax.shard_map(
        functools.partial(local, mesh.shape["seq"], mesh.shape["tensor"]),
        mesh=mesh,
        in_specs=placed,
        out_specs=(P("seq", "tensor"), P("seq", "tensor"), P("seq", "tensor", None)),
        check_vma=False,
    )
```

```python
import functools

import jax
import jax.numpy as jnp
from jax import lax
from jax.experimental import pallas as pl
from jax.experimental.pallas import tpu as pltpu
from jax.sharding import PartitionSpec as P

EPSILON = 1e-05
MESH = pl.DeviceIdType.MESH
F32 = jnp.float32
BF16 = jnp.bfloat16
ROWS = (((1,), (1,)), ((), ()))
COLUMNS = (((0,), (0,)), ((), ()))


def inverse_of(values):
    return lax.rsqrt(jnp.mean(values * values, axis=-1, keepdims=True) + EPSILON)


def dot(a, b, dims=None):
    if dims is None:
        return jnp.dot(a, b, preferred_element_type=F32)
    return lax.dot_general(a, b, dims, preferred_element_type=F32)


def kernel(
    seq_count, tensor_count,
    images_hbm, spans_hbm, query_gain_hbm, key_gain_hbm, kv_hbm, q_hbm, do_hbm,
    att_hbm, qg_hbm, kvg_hbm,
    images_ref, spans_ref, query_gain_ref, key_gain_ref, kv, q, do, qhat, send, arrive, gsend, garrive, khat, wf, gp, wb, dsb, att, qg, kvg, denoms,
    in_sem, out_sem, send_sem, recv_sem, gsend_sem, grecv_sem,
):
    s = lax.axis_index("seq")
    t = lax.axis_index("tensor")
    slots, _, sub, width2 = arrive.shape
    width = width2 // 2
    image_count = kv.shape[0]
    tokens = q.shape[0]
    group = q.shape[1] // width
    image_rows = tensor_count * sub
    all_rows = slots * image_rows
    scale = width ** (-0.5)

    def ring(k):
        return lax.rem(t + k, tensor_count)

    kv_in = pltpu.make_async_copy(kv_hbm, kv, in_sem.at[0])
    q_in = pltpu.make_async_copy(q_hbm, q, in_sem.at[1])
    do_in = pltpu.make_async_copy(do_hbm, do, in_sem.at[2])
    small = (
        (images_hbm, images_ref), (spans_hbm, spans_ref),
        (query_gain_hbm, query_gain_ref), (key_gain_hbm, key_gain_ref),
    )
    small_in = [
        pltpu.make_async_copy(a, b, in_sem.at[3 + i]) for i, (a, b) in enumerate(small)
    ]
    small_in[0].start()
    kv_in.start()
    for copy in small_in[1:]:
        copy.start()
    q_in.start()
    do_in.start()

    barrier = pltpu.get_barrier_semaphore()
    for shift in range(1 - slots, slots):

        def greet(shift=shift):
            for k in range(tensor_count):
                if shift or k:
                    pl.semaphore_signal(
                        barrier, inc=1, device_id=(s + shift, ring(k)), device_id_type=MESH
                    )

        if shift == 0:
            greet()
        else:
            pl.when((s + shift >= 0) & (s + shift < seq_count))(greet)

    small_in[0].wait()
    picks = []
    for r in range(slots):
        reader = jnp.minimum(s + r, seq_count - 1)
        pick = images_ref[r, reader] - s * image_count
        picks.append(jnp.clip(pick, 0, image_count - 1))

    kv_in.wait()
    for r in range(slots):
        chosen = kv[picks[r]]
        for k in range(tensor_count):
            send[r, k] = chosen[:, k * width2 : (k + 1) * width2]
    arrive[0, t] = send[0, t]
    for r in range(1, slots):

        @pl.when(s < r)
        def _(r=r):
            arrive[r] = jnp.zeros(arrive.shape[1:], BF16)

        @pl.when(s + r >= seq_count)
        def _(r=r):
            garrive[r] = jnp.zeros(garrive.shape[1:], BF16)

    near = jnp.minimum(s, slots - 1) + jnp.minimum(seq_count - 1 - s, slots - 1) + 1
    pl.semaphore_wait(barrier, near * tensor_count - 1)

    def forward(r, k, slot):
        return pltpu.make_async_remote_copy(
            src_ref=send.at[r, ring(k)], dst_ref=arrive.at[r, slot],
            send_sem=send_sem.at[r, k], recv_sem=recv_sem.at[r, k],
            device_id=(s + r, ring(k)), device_id_type=MESH,
        )

    def backward(r, k, slot):
        return pltpu.make_async_remote_copy(
            src_ref=gsend.at[r, ring(k)], dst_ref=garrive.at[r, slot],
            send_sem=gsend_sem.at[r, k], recv_sem=grecv_sem.at[r, k],
            device_id=(s - r, ring(k)), device_id_type=MESH,
        )

    def each(r, condition, body):
        def run():
            for k in reversed(range(tensor_count)):
                if r or k:
                    body(k)

        if r == 0:
            run()
        else:
            pl.when(condition)(run)

    def from_ring(k):
        return lax.rem(t + tensor_count - k, tensor_count)

    for r in reversed(range(slots)):
        each(r, s + r < seq_count, lambda k, r=r: forward(r, k, t).start())

    for copy in small_in[1:]:
        copy.wait()
    query_gain = query_gain_ref[...]
    key_gain = key_gain_ref[...]
    q_in.wait()
    for a in range(group):
        qf = q[:, a * width : (a + 1) * width].astype(F32)
        qhat[a] = (qf * inverse_of(qf) * query_gain).astype(BF16)
    do_in.wait()

    begins = spans_ref[0:1, :]
    ends = spans_ref[1:2, :]
    masks = [((begins <= r) & (r < ends)).astype(F32) for r in range(slots)]
    no_image = 1.0 - functools.reduce(jnp.maximum, masks)

    totals = [no_image] * group
    dots = [jnp.zeros((1, tokens), F32)] * group
    for r in range(slots):
        each(r, s >= r, lambda k, r=r: forward(r, k, from_ring(k)).wait_recv())
        rows = slice(r * image_rows, (r + 1) * image_rows)
        keys = arrive[r, :, :, :width].reshape(image_rows, width).astype(F32)
        value = arrive[r, :, :, width:].reshape(image_rows, width)
        key_hat = (keys * inverse_of(keys) * key_gain).astype(BF16)
        khat[rows] = key_hat
        mask = jnp.broadcast_to(masks[r], (image_rows, tokens))
        for a in range(group):
            weights = jnp.exp(dot(key_hat, qhat[a], ROWS) * scale) * mask
            grad_probs = dot(value, do[:, a * width : (a + 1) * width], ROWS)
            totals[a] = totals[a] + jnp.sum(weights, axis=0, keepdims=True)
            dots[a] = dots[a] + jnp.sum(weights * grad_probs, axis=0, keepdims=True)
            wf[a, rows] = weights
            gp[a, rows] = grad_probs
            wb[a, rows] = weights.astype(BF16)

    for a in range(group):
        denoms[a : a + 1, :] = totals[a]
    inverses = [1.0 / total for total in totals]
    row_dots = [d * i for d, i in zip(dots, inverses)]
    for r in reversed(range(slots)):
        rows = slice(r * image_rows, (r + 1) * image_rows)
        grad_key = jnp.zeros((image_rows, width), F32)
        grad_value = jnp.zeros((image_rows, width), F32)
        for a in range(group):
            probs = wf[a, rows] * inverses[a]
            score_grad = (probs * (gp[a, rows] - row_dots[a])).astype(BF16)
            dsb[a, rows] = score_grad
            grad_key = grad_key + dot(score_grad, qhat[a])
            grad_value = grad_value + dot(probs.astype(BF16), do[:, a * width : (a + 1) * width])
        piece = (tensor_count, sub, width)
        gsend[r, :, :, :width] = (grad_key * scale).astype(BF16).reshape(piece)
        gsend[r, :, :, width:] = grad_value.astype(BF16).reshape(piece)
        each(r, s >= r, lambda k, r=r: backward(r, k, t).start())
    key_hat = khat[...]
    values = arrive[:, :, :, width:].reshape(all_rows, width)
    garrive[0, t] = gsend[0, t]

    padded = jnp.concatenate(
        [denoms[...], jnp.ones((tokens - group, tokens), F32)], axis=0
    ) if tokens > group else denoms[...]
    columns = 1.0 / jnp.transpose(padded)
    for a in range(group):
        part = slice(a * width, (a + 1) * width)
        numerator = dot(wb[a], values, COLUMNS)
        att[:, part] = (numerator * columns[:, a : a + 1]).astype(BF16)
    att_out = pltpu.make_async_copy(att, att_hbm, out_sem.at[0])
    att_out.start()
    for a in range(group):
        part = slice(a * width, (a + 1) * width)
        scaled = query_gain * (dot(dsb[a], key_hat, COLUMNS) * scale)
        qf = q[:, part].astype(F32)
        inverse = inverse_of(qf)
        mean = jnp.mean(qf * scaled, axis=-1, keepdims=True)
        qg[:, part] = (inverse * scaled - qf * (inverse * inverse * inverse * mean)).astype(BF16)
    qg_out = pltpu.make_async_copy(qg, qg_hbm, out_sem.at[1])
    qg_out.start()

    for r in range(slots):
        each(r, s + r < seq_count, lambda k, r=r: backward(r, k, from_ring(k)).wait_recv())

    for i in range(image_count):
        chosen = [(picks[r] == i) & (s + r < seq_count) for r in range(slots)]
        for h in range(tensor_count):
            total = jnp.zeros((sub, width2), F32)
            for r in range(slots):
                total = total + jnp.where(chosen[r], garrive[r, h].astype(F32), 0.0)
            start = h * width2
            raw = kv[i, :, start : start + width].astype(F32)
            inverse = inverse_of(raw)
            scaled = key_gain * total[:, :width]
            mean = jnp.mean(raw * scaled, axis=-1, keepdims=True)
            kvg[i, :, start : start + width] = (
                inverse * scaled - raw * (inverse * inverse * inverse * mean)
            ).astype(BF16)
            kvg[i, :, start + width : start + width2] = total[:, width:].astype(BF16)
    kvg_out = pltpu.make_async_copy(kvg, kvg_hbm, out_sem.at[2])
    kvg_out.start()

    for r in range(slots):
        each(r, s + r < seq_count, lambda k, r=r: forward(r, k, t).wait_send())
        each(r, s >= r, lambda k, r=r: backward(r, k, t).wait_send())
    att_out.wait()
    qg_out.wait()
    kvg_out.wait()


def hand_out(att_in, qg_in, kvg_in, att, qg, kvg, sems):
    pairs = ((att_in, att), (qg_in, qg), (kvg_in, kvg))
    copies = [pltpu.make_async_copy(a, b, sems.at[i]) for i, (a, b) in enumerate(pairs)]
    for copy in copies:
        copy.start()
    for copy in copies:
        copy.wait()


def local(seq_count, tensor_count, queries, keyvals, reader_images, read_spans, query_gain, key_gain, out_grad):
    width = query_gain.shape[0]
    tokens, columns = queries.shape
    group = columns // width
    image_count, sub, _ = keyvals.shape
    slots = reader_images.shape[1]
    rows = slots * tensor_count * sub
    pieces = (slots, tensor_count, sub, 2 * width)
    held = pl.BlockSpec(memory_space=pltpu.HBM)
    placed = pl.BlockSpec(memory_space=pl.ANY)
    pairs = (slots, tensor_count)
    operands = (
        reader_images.T, read_spans, query_gain.reshape(1, width), key_gain.reshape(1, width),
        keyvals, queries, out_grad,
    )
    results = pl.pallas_call(
        functools.partial(kernel, seq_count, tensor_count),
        out_shape=(
            jax.ShapeDtypeStruct(queries.shape, BF16),
            jax.ShapeDtypeStruct(queries.shape, BF16),
            jax.ShapeDtypeStruct(keyvals.shape, BF16),
        ),
        in_specs=[held] * 7,
        out_specs=(placed, placed, placed),
        scratch_shapes=[
            pltpu.SMEM(reader_images.shape[::-1], jnp.int32),
            pltpu.VMEM(read_spans.shape, jnp.int32),
            pltpu.VMEM((1, width), F32),
            pltpu.VMEM((1, width), F32),
            pltpu.VMEM(keyvals.shape, BF16),
            pltpu.VMEM(queries.shape, BF16),
            pltpu.VMEM(queries.shape, BF16),
            pltpu.VMEM((group, tokens, width), BF16),
            pltpu.VMEM(pieces, BF16),
            pltpu.VMEM(pieces, BF16),
            pltpu.VMEM(pieces, BF16),
            pltpu.VMEM(pieces, BF16),
            pltpu.VMEM((rows, width), BF16),
            pltpu.VMEM((group, rows, tokens), F32),
            pltpu.VMEM((group, rows, tokens), F32),
            pltpu.VMEM((group, rows, tokens), BF16),
            pltpu.VMEM((group, rows, tokens), BF16),
            pltpu.VMEM(queries.shape, BF16),
            pltpu.VMEM(queries.shape, BF16),
            pltpu.VMEM(keyvals.shape, BF16),
            pltpu.VMEM((group, tokens), F32),
            pltpu.SemaphoreType.DMA((7,)),
            pltpu.SemaphoreType.DMA((3,)),
            pltpu.SemaphoreType.DMA(pairs),
            pltpu.SemaphoreType.DMA(pairs),
            pltpu.SemaphoreType.DMA(pairs),
            pltpu.SemaphoreType.DMA(pairs),
        ],
        compiler_params=pltpu.CompilerParams(collective_id=0, has_side_effects=True, vmem_limit_bytes=24 * 2**20),
        name="cross_attention",
    )(*[pltpu.with_memory_space_constraint(operand, pltpu.HBM) for operand in operands])
    return pl.pallas_call(
        hand_out,
        out_shape=tuple(jax.ShapeDtypeStruct(r.shape, r.dtype) for r in results),
        in_specs=[placed] * len(results),
        out_specs=(placed,) * len(results),
        scratch_shapes=[pltpu.SemaphoreType.DMA((len(results),))],
        compiler_params=pltpu.CompilerParams(vmem_limit_bytes=2**20),
        name="hand_out",
    )(*results)


def solution(mesh):
    placed = (
        P("seq", "tensor"),
        P("seq", "tensor", None),
        P(),
        P(None, "seq"),
        P(),
        P(),
        P("seq", "tensor"),
    )
    return jax.shard_map(
        functools.partial(local, mesh.shape["seq"], mesh.shape["tensor"]),
        mesh=mesh,
        in_specs=placed,
        out_specs=(P("seq", "tensor"), P("seq", "tensor"), P("seq", "tensor", None)),
        check_vma=False,
    )
```

```python
import functools

import jax
import jax.numpy as jnp
from jax import lax
from jax.experimental import pallas as pl
from jax.experimental.pallas import tpu as pltpu
from jax.sharding import PartitionSpec as P

EPSILON = 1e-05
MESH = pl.DeviceIdType.MESH
F32 = jnp.float32
BF16 = jnp.bfloat16
ROWS = (((1,), (1,)), ((), ()))
COLUMNS = (((0,), (0,)), ((), ()))


def inverse_of(values):
    return lax.rsqrt(jnp.mean(values * values, axis=-1, keepdims=True) + EPSILON)


def dot(a, b, dims=None):
    if dims is None:
        return jnp.dot(a, b, preferred_element_type=F32)
    return lax.dot_general(a, b, dims, preferred_element_type=F32)


def kernel(
    seq_count, tensor_count,
    images_hbm, spans_hbm, query_gain_hbm, key_gain_hbm, kv_hbm, q_hbm, do_hbm,
    att_hbm, qg_hbm, kvg_hbm,
    images_ref, spans_ref, query_gain_ref, key_gain_ref, kv, q, do, qhat, send, arrive, gsend, garrive, khat, wf, gp, wb, dsb, att, qg, kvg, denoms, gains, cubes, products, sums,
    in_sem, out_sem, send_sem, recv_sem, gsend_sem, grecv_sem,
):
    s = lax.axis_index("seq")
    t = lax.axis_index("tensor")
    slots, _, sub, width2 = arrive.shape
    width = width2 // 2
    image_count = kv.shape[0]
    tokens = q.shape[0]
    group = q.shape[1] // width
    image_rows = tensor_count * sub
    all_rows = slots * image_rows
    scale = width ** (-0.5)

    def ring(k):
        return lax.rem(t + k, tensor_count)

    kv_in = pltpu.make_async_copy(kv_hbm, kv, in_sem.at[0])
    q_in = pltpu.make_async_copy(q_hbm, q, in_sem.at[1])
    do_in = pltpu.make_async_copy(do_hbm, do, in_sem.at[2])
    small = (
        (images_hbm, images_ref), (spans_hbm, spans_ref),
        (query_gain_hbm, query_gain_ref), (key_gain_hbm, key_gain_ref),
    )
    small_in = [
        pltpu.make_async_copy(a, b, in_sem.at[3 + i]) for i, (a, b) in enumerate(small)
    ]
    small_in[0].start()
    kv_in.start()
    for copy in small_in[1:]:
        copy.start()
    q_in.start()
    do_in.start()

    barrier = pltpu.get_barrier_semaphore()
    for shift in range(1 - slots, slots):

        def greet(shift=shift):
            for k in range(tensor_count):
                if shift or k:
                    pl.semaphore_signal(
                        barrier, inc=1, device_id=(s + shift, ring(k)), device_id_type=MESH
                    )

        if shift == 0:
            greet()
        else:
            pl.when((s + shift >= 0) & (s + shift < seq_count))(greet)

    small_in[0].wait()
    picks = []
    for r in range(slots):
        reader = jnp.minimum(s + r, seq_count - 1)
        pick = images_ref[r, reader] - s * image_count
        picks.append(jnp.clip(pick, 0, image_count - 1))

    kv_in.wait()
    for r in range(slots):
        chosen = kv[picks[r]]
        for k in range(tensor_count):
            send[r, k] = chosen[:, k * width2 : (k + 1) * width2]
    arrive[0, t] = send[0, t]
    for r in range(1, slots):

        @pl.when(s < r)
        def _(r=r):
            arrive[r] = jnp.zeros(arrive.shape[1:], BF16)

        @pl.when(s + r >= seq_count)
        def _(r=r):
            garrive[r] = jnp.zeros(garrive.shape[1:], BF16)

    near = jnp.minimum(s, slots - 1) + jnp.minimum(seq_count - 1 - s, slots - 1) + 1
    pl.semaphore_wait(barrier, near * tensor_count - 1)

    def forward(r, k, slot):
        return pltpu.make_async_remote_copy(
            src_ref=send.at[r, ring(k)], dst_ref=arrive.at[r, slot],
            send_sem=send_sem.at[r, k], recv_sem=recv_sem.at[r, k],
            device_id=(s + r, ring(k)), device_id_type=MESH,
        )

    def backward(r, k, slot):
        return pltpu.make_async_remote_copy(
            src_ref=gsend.at[r, ring(k)], dst_ref=garrive.at[r, slot],
            send_sem=gsend_sem.at[r, k], recv_sem=grecv_sem.at[r, k],
            device_id=(s - r, ring(k)), device_id_type=MESH,
        )

    def each(r, condition, body):
        def run():
            for k in reversed(range(tensor_count)):
                if r or k:
                    body(k)

        if r == 0:
            run()
        else:
            pl.when(condition)(run)

    def from_ring(k):
        return lax.rem(t + tensor_count - k, tensor_count)

    for r in reversed(range(slots)):
        each(r, s + r < seq_count, lambda k, r=r: forward(r, k, t).start())

    for copy in small_in[1:]:
        copy.wait()
    query_gain = query_gain_ref[...]
    key_gain = key_gain_ref[...]
    q_in.wait()
    for a in range(group):
        qf = q[:, a * width : (a + 1) * width].astype(F32)
        qhat[a] = (qf * inverse_of(qf) * query_gain).astype(BF16)
    do_in.wait()

    begins = spans_ref[0:1, :]
    ends = spans_ref[1:2, :]
    masks = [((begins <= r) & (r < ends)).astype(F32) for r in range(slots)]
    no_image = 1.0 - functools.reduce(jnp.maximum, masks)

    totals = [no_image] * group
    dots = [jnp.zeros((1, tokens), F32)] * group
    for r in range(slots):
        each(r, s >= r, lambda k, r=r: forward(r, k, from_ring(k)).wait_recv())
        rows = slice(r * image_rows, (r + 1) * image_rows)
        keys = arrive[r, :, :, :width].reshape(image_rows, width).astype(F32)
        value = arrive[r, :, :, width:].reshape(image_rows, width)
        key_hat = (keys * inverse_of(keys) * key_gain).astype(BF16)
        khat[rows] = key_hat
        mask = jnp.broadcast_to(masks[r], (image_rows, tokens))
        for a in range(group):
            weights = jnp.exp(dot(key_hat, qhat[a], ROWS) * scale) * mask
            grad_probs = dot(value, do[:, a * width : (a + 1) * width], ROWS)
            totals[a] = totals[a] + jnp.sum(weights, axis=0, keepdims=True)
            dots[a] = dots[a] + jnp.sum(weights * grad_probs, axis=0, keepdims=True)
            wf[a, rows] = weights
            gp[a, rows] = grad_probs
            wb[a, rows] = weights.astype(BF16)

    for a in range(group):
        denoms[a : a + 1, :] = totals[a]
    inverses = [1.0 / total for total in totals]
    row_dots = [d * i for d, i in zip(dots, inverses)]
    for r in reversed(range(slots)):
        rows = slice(r * image_rows, (r + 1) * image_rows)
        grad_key = jnp.zeros((image_rows, width), F32)
        grad_value = jnp.zeros((image_rows, width), F32)
        for a in range(group):
            probs = wf[a, rows] * inverses[a]
            score_grad = (probs * (gp[a, rows] - row_dots[a])).astype(BF16)
            dsb[a, rows] = score_grad
            grad_key = grad_key + dot(score_grad, qhat[a])
            grad_value = grad_value + dot(probs.astype(BF16), do[:, a * width : (a + 1) * width])
        piece = (tensor_count, sub, width)
        gsend[r, :, :, :width] = (grad_key * scale).astype(BF16).reshape(piece)
        gsend[r, :, :, width:] = grad_value.astype(BF16).reshape(piece)
        each(r, s >= r, lambda k, r=r: backward(r, k, t).start())
    key_hat = khat[...]
    values = arrive[:, :, :, width:].reshape(all_rows, width)
    garrive[0, t] = gsend[0, t]

    padded = jnp.concatenate(
        [denoms[...], jnp.ones((tokens - group, tokens), F32)], axis=0
    ) if tokens > group else denoms[...]
    columns = 1.0 / jnp.transpose(padded)
    for a in range(group):
        part = slice(a * width, (a + 1) * width)
        numerator = dot(wb[a], values, COLUMNS)
        att[:, part] = (numerator * columns[:, a : a + 1]).astype(BF16)
    att_out = pltpu.make_async_copy(att, att_hbm, out_sem.at[0])
    att_out.start()
    for a in range(group):
        part = slice(a * width, (a + 1) * width)
        scaled = query_gain * (dot(dsb[a], key_hat, COLUMNS) * scale)
        qf = q[:, part].astype(F32)
        inverse = inverse_of(qf)
        mean = jnp.mean(qf * scaled, axis=-1, keepdims=True)
        qg[:, part] = (inverse * scaled - qf * (inverse * inverse * inverse * mean)).astype(BF16)
    qg_out = pltpu.make_async_copy(qg, qg_hbm, out_sem.at[1])
    qg_out.start()

    for i in range(image_count):
        for h in range(tensor_count):
            start = h * width2
            raw = kv[i, :, start : start + width].astype(F32)
            inverse = inverse_of(raw)
            gains[i, h] = key_gain * inverse
            cubes[i, h] = raw * (inverse * inverse * inverse)
            products[i, h] = raw * key_gain

    chosen = [
        [(picks[r] == i) & (s + r < seq_count) for r in range(slots)]
        for i in range(image_count)
    ]

    def taken(i, h, r):
        return jnp.where(chosen[i][r], garrive[r, h].astype(F32), 0.0)

    for r in range(slots):
        each(r, s + r < seq_count, lambda k, r=r: backward(r, k, from_ring(k)).wait_recv())
        if r + 1 == slots:
            break
        for i in range(image_count):
            for h in range(tensor_count):
                sums[i, h] = taken(i, h, r) + (sums[i, h] if r else 0.0)

    kvg_out = []
    for i in range(image_count):
        for h in range(tensor_count):
            total = taken(i, h, slots - 1) + (sums[i, h] if slots > 1 else 0.0)
            start = h * width2
            grad = total[:, :width]
            mean = jnp.mean(products[i, h] * grad, axis=-1, keepdims=True)
            kvg[i, :, start : start + width] = (
                gains[i, h] * grad - cubes[i, h] * mean
            ).astype(BF16)
            kvg[i, :, start + width : start + width2] = total[:, width:].astype(BF16)
        kvg_out.append(pltpu.make_async_copy(kvg.at[i], kvg_hbm.at[i], out_sem.at[2 + i]))
        kvg_out[i].start()

    for r in range(slots):
        each(r, s + r < seq_count, lambda k, r=r: forward(r, k, t).wait_send())
        each(r, s >= r, lambda k, r=r: backward(r, k, t).wait_send())
    att_out.wait()
    qg_out.wait()
    for copy in kvg_out:
        copy.wait()


def hand_out(att_in, qg_in, kvg_in, att, qg, kvg, sems):
    copies = []
    for source, target in ((att_in, att), (qg_in, qg), (kvg_in, kvg)):
        count = source.shape[0]
        cuts = min(sems.shape[1], count)
        size = -(-count // cuts)
        for start in range(0, count, size):
            part = pl.ds(start, min(size, count - start))
            sem = sems.at[len(copies) // sems.shape[1], len(copies) % sems.shape[1]]
            copies.append(pltpu.make_async_copy(source.at[part], target.at[part], sem))
            copies[-1].start()
    for copy in copies:
        copy.wait()


def local(seq_count, tensor_count, queries, keyvals, reader_images, read_spans, query_gain, key_gain, out_grad):
    width = query_gain.shape[0]
    tokens, columns = queries.shape
    group = columns // width
    image_count, sub, _ = keyvals.shape
    slots = reader_images.shape[1]
    rows = slots * tensor_count * sub
    pieces = (slots, tensor_count, sub, 2 * width)
    held = pl.BlockSpec(memory_space=pltpu.HBM)
    placed = pl.BlockSpec(memory_space=pl.ANY)
    pairs = (slots, tensor_count)
    operands = (
        reader_images.T, read_spans, query_gain.reshape(1, width), key_gain.reshape(1, width),
        keyvals, queries, out_grad,
    )
    results = pl.pallas_call(
        functools.partial(kernel, seq_count, tensor_count),
        out_shape=(
            jax.ShapeDtypeStruct(queries.shape, BF16),
            jax.ShapeDtypeStruct(queries.shape, BF16),
            jax.ShapeDtypeStruct(keyvals.shape, BF16),
        ),
        in_specs=[held] * 7,
        out_specs=(placed, placed, placed),
        scratch_shapes=[
            pltpu.SMEM(reader_images.shape[::-1], jnp.int32),
            pltpu.VMEM(read_spans.shape, jnp.int32),
            pltpu.VMEM((1, width), F32),
            pltpu.VMEM((1, width), F32),
            pltpu.VMEM(keyvals.shape, BF16),
            pltpu.VMEM(queries.shape, BF16),
            pltpu.VMEM(queries.shape, BF16),
            pltpu.VMEM((group, tokens, width), BF16),
            pltpu.VMEM(pieces, BF16),
            pltpu.VMEM(pieces, BF16),
            pltpu.VMEM(pieces, BF16),
            pltpu.VMEM(pieces, BF16),
            pltpu.VMEM((rows, width), BF16),
            pltpu.VMEM((group, rows, tokens), F32),
            pltpu.VMEM((group, rows, tokens), F32),
            pltpu.VMEM((group, rows, tokens), BF16),
            pltpu.VMEM((group, rows, tokens), BF16),
            pltpu.VMEM(queries.shape, BF16),
            pltpu.VMEM(queries.shape, BF16),
            pltpu.VMEM(keyvals.shape, BF16),
            pltpu.VMEM((group, tokens), F32),
            pltpu.VMEM((image_count, tensor_count, sub, width), F32),
            pltpu.VMEM((image_count, tensor_count, sub, width), F32),
            pltpu.VMEM((image_count, tensor_count, sub, width), F32),
            pltpu.VMEM((image_count, tensor_count, sub, 2 * width), F32),
            pltpu.SemaphoreType.DMA((7,)),
            pltpu.SemaphoreType.DMA((2 + image_count,)),
            pltpu.SemaphoreType.DMA(pairs),
            pltpu.SemaphoreType.DMA(pairs),
            pltpu.SemaphoreType.DMA(pairs),
            pltpu.SemaphoreType.DMA(pairs),
        ],
        compiler_params=pltpu.CompilerParams(collective_id=0, has_side_effects=True, vmem_limit_bytes=24 * 2**20),
        name="cross_attention",
    )(*[pltpu.with_memory_space_constraint(operand, pltpu.HBM) for operand in operands])
    return pl.pallas_call(
        hand_out,
        out_shape=tuple(jax.ShapeDtypeStruct(r.shape, r.dtype) for r in results),
        in_specs=[placed] * len(results),
        out_specs=(placed,) * len(results),
        scratch_shapes=[pltpu.SemaphoreType.DMA((len(results), 4))],
        compiler_params=pltpu.CompilerParams(vmem_limit_bytes=2**20),
        name="hand_out",
    )(*results)


def solution(mesh):
    placed = (
        P("seq", "tensor"),
        P("seq", "tensor", None),
        P(),
        P(None, "seq"),
        P(),
        P(),
        P("seq", "tensor"),
    )
    return jax.shard_map(
        functools.partial(local, mesh.shape["seq"], mesh.shape["tensor"]),
        mesh=mesh,
        in_specs=placed,
        out_specs=(P("seq", "tensor"), P("seq", "tensor"), P("seq", "tensor", None)),
        check_vma=False,
    )
```

```python
import functools

import jax
import jax.numpy as jnp
from jax import lax
from jax.experimental import pallas as pl
from jax.experimental.pallas import tpu as pltpu
from jax.sharding import PartitionSpec as P

EPSILON = 1e-05
MESH = pl.DeviceIdType.MESH
F32 = jnp.float32
BF16 = jnp.bfloat16
ROWS = (((1,), (1,)), ((), ()))
COLUMNS = (((0,), (0,)), ((), ()))


def inverse_of(values):
    return lax.rsqrt(jnp.mean(values * values, axis=-1, keepdims=True) + EPSILON)


def dot(a, b, dims=None):
    if dims is None:
        return jnp.dot(a, b, preferred_element_type=F32)
    return lax.dot_general(a, b, dims, preferred_element_type=F32)


def kernel(
    seq_count, tensor_count,
    images_hbm, spans_hbm, query_gain_hbm, key_gain_hbm, kv_hbm, q_hbm, do_hbm,
    att_hbm, qg_hbm, kvg_hbm,
    images_ref, spans_ref, query_gain_ref, key_gain_ref, kv, q, do, qhat, send, arrive, gsend, garrive, khat, wf, gp, wb, dsb, att, qg, kvg, denoms, gains, cubes, products, sums,
    in_sem, out_sem, send_sem, recv_sem, gsend_sem, grecv_sem,
):
    s = lax.axis_index("seq")
    t = lax.axis_index("tensor")
    slots, _, sub, width2 = arrive.shape
    width = width2 // 2
    image_count = kv.shape[0]
    tokens = q.shape[0]
    group = q.shape[1] // width
    image_rows = tensor_count * sub
    all_rows = slots * image_rows
    scale = width ** (-0.5)

    def ring(k):
        return lax.rem(t + k, tensor_count)

    kv_in = pltpu.make_async_copy(kv_hbm, kv, in_sem.at[0])
    q_in = pltpu.make_async_copy(q_hbm, q, in_sem.at[1])
    do_in = pltpu.make_async_copy(do_hbm, do, in_sem.at[2])
    small = (
        (images_hbm, images_ref), (spans_hbm, spans_ref),
        (query_gain_hbm, query_gain_ref), (key_gain_hbm, key_gain_ref),
    )
    small_in = [
        pltpu.make_async_copy(a, b, in_sem.at[3 + i]) for i, (a, b) in enumerate(small)
    ]
    small_in[0].start()
    kv_in.start()
    for copy in small_in[1:]:
        copy.start()
    q_in.start()
    do_in.start()

    barrier = pltpu.get_barrier_semaphore()
    for shift in range(1 - slots, slots):

        def greet(shift=shift):
            for k in range(tensor_count):
                if shift or k:
                    pl.semaphore_signal(
                        barrier, inc=1, device_id=(s + shift, ring(k)), device_id_type=MESH
                    )

        if shift == 0:
            greet()
        else:
            pl.when((s + shift >= 0) & (s + shift < seq_count))(greet)

    small_in[0].wait()
    picks = []
    for r in range(slots):
        reader = jnp.minimum(s + r, seq_count - 1)
        pick = images_ref[r, reader] - s * image_count
        picks.append(jnp.clip(pick, 0, image_count - 1))

    kv_in.wait()
    for r in range(slots):
        chosen = kv[picks[r]]
        for k in range(tensor_count):
            send[r, k] = chosen[:, k * width2 : (k + 1) * width2]
    arrive[0, t] = send[0, t]
    for r in range(1, slots):

        @pl.when(s < r)
        def _(r=r):
            arrive[r] = jnp.zeros(arrive.shape[1:], BF16)

        @pl.when(s + r >= seq_count)
        def _(r=r):
            garrive[r] = jnp.zeros(garrive.shape[1:], BF16)

    near = jnp.minimum(s, slots - 1) + jnp.minimum(seq_count - 1 - s, slots - 1) + 1
    pl.semaphore_wait(barrier, near * tensor_count - 1)

    def forward(r, k, slot):
        return pltpu.make_async_remote_copy(
            src_ref=send.at[r, ring(k)], dst_ref=arrive.at[r, slot],
            send_sem=send_sem.at[r, k], recv_sem=recv_sem.at[r, k],
            device_id=(s + r, ring(k)), device_id_type=MESH,
        )

    def backward(r, k, slot):
        return pltpu.make_async_remote_copy(
            src_ref=gsend.at[r, ring(k)], dst_ref=garrive.at[r, slot],
            send_sem=gsend_sem.at[r, k], recv_sem=grecv_sem.at[r, k],
            device_id=(s - r, ring(k)), device_id_type=MESH,
        )

    def each(r, condition, body):
        def run():
            for k in reversed(range(tensor_count)):
                if r or k:
                    body(k)

        if r == 0:
            run()
        else:
            pl.when(condition)(run)

    def from_ring(k):
        return lax.rem(t + tensor_count - k, tensor_count)

    for r in reversed(range(slots)):
        each(r, s + r < seq_count, lambda k, r=r: forward(r, k, t).start())

    for copy in small_in[1:]:
        copy.wait()
    query_gain = query_gain_ref[...]
    key_gain = key_gain_ref[...]
    q_in.wait()
    for a in range(group):
        qf = q[:, a * width : (a + 1) * width].astype(F32)
        qhat[a] = (qf * inverse_of(qf) * query_gain).astype(BF16)
    do_in.wait()

    begins = spans_ref[0:1, :]
    ends = spans_ref[1:2, :]
    masks = [((begins <= r) & (r < ends)).astype(F32) for r in range(slots)]
    no_image = 1.0 - functools.reduce(jnp.maximum, masks)

    totals = [no_image] * group
    dots = [jnp.zeros((1, tokens), F32)] * group
    for r in (0, *range(slots - 1, 0, -1)):
        each(r, s >= r, lambda k, r=r: forward(r, k, from_ring(k)).wait_recv())
        rows = slice(r * image_rows, (r + 1) * image_rows)
        keys = arrive[r, :, :, :width].reshape(image_rows, width).astype(F32)
        value = arrive[r, :, :, width:].reshape(image_rows, width)
        key_hat = (keys * inverse_of(keys) * key_gain).astype(BF16)
        khat[rows] = key_hat
        mask = jnp.broadcast_to(masks[r], (image_rows, tokens))
        for a in range(group):
            weights = jnp.exp(dot(key_hat, qhat[a], ROWS) * scale) * mask
            grad_probs = dot(value, do[:, a * width : (a + 1) * width], ROWS)
            totals[a] = totals[a] + jnp.sum(weights, axis=0, keepdims=True)
            dots[a] = dots[a] + jnp.sum(weights * grad_probs, axis=0, keepdims=True)
            wf[a, rows] = weights
            gp[a, rows] = grad_probs
            wb[a, rows] = weights.astype(BF16)

    for a in range(group):
        denoms[a : a + 1, :] = totals[a]
    inverses = [1.0 / total for total in totals]
    row_dots = [d * i for d, i in zip(dots, inverses)]
    for r in reversed(range(slots)):
        rows = slice(r * image_rows, (r + 1) * image_rows)
        grad_key = jnp.zeros((image_rows, width), F32)
        grad_value = jnp.zeros((image_rows, width), F32)
        for a in range(group):
            probs = wf[a, rows] * inverses[a]
            score_grad = (probs * (gp[a, rows] - row_dots[a])).astype(BF16)
            dsb[a, rows] = score_grad
            grad_key = grad_key + dot(score_grad, qhat[a])
            grad_value = grad_value + dot(probs.astype(BF16), do[:, a * width : (a + 1) * width])
        piece = (tensor_count, sub, width)
        gsend[r, :, :, :width] = (grad_key * scale).astype(BF16).reshape(piece)
        gsend[r, :, :, width:] = grad_value.astype(BF16).reshape(piece)
        each(r, s >= r, lambda k, r=r: backward(r, k, t).start())
    key_hat = khat[...]
    values = arrive[:, :, :, width:].reshape(all_rows, width)
    garrive[0, t] = gsend[0, t]

    padded = jnp.concatenate(
        [denoms[...], jnp.ones((tokens - group, tokens), F32)], axis=0
    ) if tokens > group else denoms[...]
    columns = 1.0 / jnp.transpose(padded)
    for a in range(group):
        part = slice(a * width, (a + 1) * width)
        numerator = dot(wb[a], values, COLUMNS)
        att[:, part] = (numerator * columns[:, a : a + 1]).astype(BF16)
    att_out = pltpu.make_async_copy(att, att_hbm, out_sem.at[0])
    att_out.start()
    for a in range(group):
        part = slice(a * width, (a + 1) * width)
        scaled = query_gain * (dot(dsb[a], key_hat, COLUMNS) * scale)
        qf = q[:, part].astype(F32)
        inverse = inverse_of(qf)
        mean = jnp.mean(qf * scaled, axis=-1, keepdims=True)
        qg[:, part] = (inverse * scaled - qf * (inverse * inverse * inverse * mean)).astype(BF16)
    qg_out = pltpu.make_async_copy(qg, qg_hbm, out_sem.at[1])
    qg_out.start()

    for i in range(image_count):
        for h in range(tensor_count):
            start = h * width2
            raw = kv[i, :, start : start + width].astype(F32)
            inverse = inverse_of(raw)
            gains[i, h] = key_gain * inverse
            cubes[i, h] = raw * (inverse * inverse * inverse)
            products[i, h] = raw * key_gain

    chosen = [
        [(picks[r] == i) & (s + r < seq_count) for r in range(slots)]
        for i in range(image_count)
    ]

    def taken(i, h, r):
        return jnp.where(chosen[i][r], garrive[r, h].astype(F32), 0.0)

    for r in range(slots):
        each(r, s + r < seq_count, lambda k, r=r: backward(r, k, from_ring(k)).wait_recv())
        if r + 1 == slots:
            break
        for i in range(image_count):
            for h in range(tensor_count):
                sums[i, h] = taken(i, h, r) + (sums[i, h] if r else 0.0)

    kvg_out = []
    for i in range(image_count):
        for h in range(tensor_count):
            total = taken(i, h, slots - 1) + (sums[i, h] if slots > 1 else 0.0)
            start = h * width2
            grad = total[:, :width]
            mean = jnp.mean(products[i, h] * grad, axis=-1, keepdims=True)
            kvg[i, :, start : start + width] = (
                gains[i, h] * grad - cubes[i, h] * mean
            ).astype(BF16)
            kvg[i, :, start + width : start + width2] = total[:, width:].astype(BF16)
        kvg_out.append(pltpu.make_async_copy(kvg.at[i], kvg_hbm.at[i], out_sem.at[2 + i]))
        kvg_out[i].start()

    for r in range(slots):
        each(r, s + r < seq_count, lambda k, r=r: forward(r, k, t).wait_send())
        each(r, s >= r, lambda k, r=r: backward(r, k, t).wait_send())
    att_out.wait()
    qg_out.wait()
    for copy in kvg_out:
        copy.wait()


def hand_out(att_in, qg_in, kvg_in, att, qg, kvg, sems):
    copies = []
    for source, target in ((att_in, att), (qg_in, qg), (kvg_in, kvg)):
        count = source.shape[0]
        cuts = min(sems.shape[1], count)
        size = -(-count // cuts)
        for start in range(0, count, size):
            part = pl.ds(start, min(size, count - start))
            sem = sems.at[len(copies) // sems.shape[1], len(copies) % sems.shape[1]]
            copies.append(pltpu.make_async_copy(source.at[part], target.at[part], sem))
            copies[-1].start()
    for copy in copies:
        copy.wait()


def local(seq_count, tensor_count, queries, keyvals, reader_images, read_spans, query_gain, key_gain, out_grad):
    width = query_gain.shape[0]
    tokens, columns = queries.shape
    group = columns // width
    image_count, sub, _ = keyvals.shape
    slots = reader_images.shape[1]
    rows = slots * tensor_count * sub
    pieces = (slots, tensor_count, sub, 2 * width)
    held = pl.BlockSpec(memory_space=pltpu.HBM)
    placed = pl.BlockSpec(memory_space=pl.ANY)
    pairs = (slots, tensor_count)
    operands = (
        reader_images.T, read_spans, query_gain.reshape(1, width), key_gain.reshape(1, width),
        keyvals, queries, out_grad,
    )
    results = pl.pallas_call(
        functools.partial(kernel, seq_count, tensor_count),
        out_shape=(
            jax.ShapeDtypeStruct(queries.shape, BF16),
            jax.ShapeDtypeStruct(queries.shape, BF16),
            jax.ShapeDtypeStruct(keyvals.shape, BF16),
        ),
        in_specs=[held] * 7,
        out_specs=(placed, placed, placed),
        scratch_shapes=[
            pltpu.SMEM(reader_images.shape[::-1], jnp.int32),
            pltpu.VMEM(read_spans.shape, jnp.int32),
            pltpu.VMEM((1, width), F32),
            pltpu.VMEM((1, width), F32),
            pltpu.VMEM(keyvals.shape, BF16),
            pltpu.VMEM(queries.shape, BF16),
            pltpu.VMEM(queries.shape, BF16),
            pltpu.VMEM((group, tokens, width), BF16),
            pltpu.VMEM(pieces, BF16),
            pltpu.VMEM(pieces, BF16),
            pltpu.VMEM(pieces, BF16),
            pltpu.VMEM(pieces, BF16),
            pltpu.VMEM((rows, width), BF16),
            pltpu.VMEM((group, rows, tokens), F32),
            pltpu.VMEM((group, rows, tokens), F32),
            pltpu.VMEM((group, rows, tokens), BF16),
            pltpu.VMEM((group, rows, tokens), BF16),
            pltpu.VMEM(queries.shape, BF16),
            pltpu.VMEM(queries.shape, BF16),
            pltpu.VMEM(keyvals.shape, BF16),
            pltpu.VMEM((group, tokens), F32),
            pltpu.VMEM((image_count, tensor_count, sub, width), F32),
            pltpu.VMEM((image_count, tensor_count, sub, width), F32),
            pltpu.VMEM((image_count, tensor_count, sub, width), F32),
            pltpu.VMEM((image_count, tensor_count, sub, 2 * width), F32),
            pltpu.SemaphoreType.DMA((7,)),
            pltpu.SemaphoreType.DMA((2 + image_count,)),
            pltpu.SemaphoreType.DMA(pairs),
            pltpu.SemaphoreType.DMA(pairs),
            pltpu.SemaphoreType.DMA(pairs),
            pltpu.SemaphoreType.DMA(pairs),
        ],
        compiler_params=pltpu.CompilerParams(collective_id=0, has_side_effects=True, vmem_limit_bytes=24 * 2**20),
        name="cross_attention",
    )(*[pltpu.with_memory_space_constraint(operand, pltpu.HBM) for operand in operands])
    return pl.pallas_call(
        hand_out,
        out_shape=tuple(jax.ShapeDtypeStruct(r.shape, r.dtype) for r in results),
        in_specs=[placed] * len(results),
        out_specs=(placed,) * len(results),
        scratch_shapes=[pltpu.SemaphoreType.DMA((len(results), 1))],
        compiler_params=pltpu.CompilerParams(vmem_limit_bytes=2**20),
        name="hand_out",
    )(*results)


def solution(mesh):
    placed = (
        P("seq", "tensor"),
        P("seq", "tensor", None),
        P(),
        P(None, "seq"),
        P(),
        P(),
        P("seq", "tensor"),
    )
    return jax.shard_map(
        functools.partial(local, mesh.shape["seq"], mesh.shape["tensor"]),
        mesh=mesh,
        in_specs=placed,
        out_specs=(P("seq", "tensor"), P("seq", "tensor"), P("seq", "tensor", None)),
        check_vma=False,
    )
```
